32 devices in a mesh: dp: 16 (over z, y, core), tensor: 2 (over x).
Axes of the slice: x: 2, y: 2, z: 4, core: 2. Of those that a mesh axis runs over, the one named last changes fastest.
Arguments:
- tokens: bfloat16 [6144, 2880], P('dp', 'tensor'), may hold values from -6 to 6
- out_grad: bfloat16 [6144, 2880], P('dp', 'tensor'), may hold values from -6 to 6
- route_probs: bfloat16 [6144, 4], P('dp'), may hold values from 0.099609375 to 1
- expert_ids: int32 [6144, 4], P('dp'), may hold values from 0 to 63, all different within a row; in each aligned block of 384 rows (0 to 383, 384 to 767, ...) at most 36 rows name the same one
- placement_map: int32 [64], replicated, may hold values from 0 to 63, each once
- w_gate: bfloat16 [16, 2880, 2880], P('dp', None, 'tensor'), may hold values from -0.109375 to 0.109375
- w_up: bfloat16 [16, 2880, 2880], P('dp', None, 'tensor'), may hold values from -0.109375 to 0.109375
- w_down: bfloat16 [16, 2880, 2880], P('dp', 'tensor'), may hold values from -0.109375 to 0.109375
Outputs:
- input_grad: bfloat16 [6144, 2880], P('dp', 'tensor')
- gate_grad: bfloat16 [16, 2880, 2880], P('dp', None, 'tensor')
- up_grad: bfloat16 [16, 2880, 2880], P('dp', None, 'tensor')
- down_grad: bfloat16 [16, 2880, 2880], P('dp', 'tensor')
- prob_grad: bfloat16 [6144, 4], P('dp')
The draws below stay inside these ranges and needn't reach their ends.
Inputs may be any that keep to these rules, and one draw needn't show every extreme that they name: `expert_ids`: each row names 4 different experts. In the rows of one index of dp no expert is named by more than 36 rows, a bound that some block reaches. `placement_map`: A permutation: every value is taken by exactly one expert.
All inputs are finite; a program needn't handle non-finite values.
Results may differ from the reference program's by a relative error of at most 0.011.
Values may be sent and summed in bfloat16 or wider, within the bound.
A program may use at most 128 MiB of HBM per device.

```python
import math
import jax
import jax.numpy as jnp
import numpy as np
from jax import lax

D = 2880
FF = 2880
TOP = 4
EXP_OWN = 4
EXPERTS = 64
TOK_DEV = 384
TOKENS = 6144
CAP = 36
N_DP = 16
N_TENSOR = 2


def steps_of(rng, dims, split, least, high):
    loudness, own = 1.0, jax.random.fold_in(rng, 6)
    for dim, blocks in split:
        draws = jnp.exp(jax.random.uniform(jax.random.fold_in(own, dim), (blocks,), jnp.float32, least / len(split), high / len(split)))
        loudness = loudness * jnp.repeat(draws, dims[dim] // blocks).reshape([-1 if axis == dim else 1 for axis in range(len(dims))])
    return loudness


def deal_out(own_key, own, number, rows, count, top, limit, slope):
    sequence = jax.random.permutation(own_key, count)
    packed, ordinary = shares(count, rows * top, limit, slope, True), shares(count, rows * top, limit, slope, False)
    places = jnp.arange(count)

    def named(tallies, offset_by):
        used = int((tallies > 0).sum())
        fixed = max(1, used // 4)
        passed = fixed + (places - fixed + offset_by * (used - fixed)) % max(1, count - fixed)
        return jnp.zeros((count,), jnp.int32).at[sequence[jnp.where(places < fixed, places, passed)]].set(jnp.asarray(tallies, jnp.int32))

    tallies = jnp.where(number % 4 == 0, named(packed, number // 4), named(ordinary, number - number // 4 - 1))
    mixed = jax.random.permutation(jax.random.fold_in(own, 3), count)
    donor, receiver = mixed[0:count // 2 * 2:2], mixed[1:count // 2 * 2:2]
    slack = jnp.minimum(tallies[donor] - 1, limit - tallies[receiver]) // 2
    slack = jnp.where((donor == sequence[0]) | (receiver == sequence[0]) | (tallies[receiver] == 0), 0, jnp.maximum(slack, 0))
    passed = jax.random.randint(jax.random.fold_in(own, 4), (count // 2,), 0, 1 << 20) % (slack + 1)
    tallies = tallies.at[donor].add(-passed).at[receiver].add(passed)
    members = jnp.searchsorted(jnp.cumsum(tallies), jnp.arange(rows * top), side="right").astype(jnp.int32)
    table = members.reshape(top, rows).T
    table = table[jax.random.permutation(jax.random.fold_in(own, 1), rows)]
    offset_by = jax.random.randint(jax.random.fold_in(own, 2), (rows, 1), 0, top)
    return jnp.take_along_axis(table, (jnp.arange(top)[None, :] + offset_by) % top, axis=1)


def shares(amount, total, reach, slope, full):
    loads = [(1 << 20) // math.isqrt(rank ** slope) + 1 for rank in range(1, amount + 1)]
    largest = reach if full else min(reach, max(-(-total // amount), total * loads[0] // sum(loads)))
    least = 1 if total - largest >= amount - 1 else 0
    counts, surplus = [largest] + [least] * (amount - 1), total - largest - least * (amount - 1)
    while surplus > 0:
        candidates = [i for i in range(1, amount) if counts[i] < largest] or [i for i in range(1, amount) if counts[i] < reach]
        mass, left = sum([loads[i] for i in candidates]), surplus
        for i in candidates:
            extra = min(reach - counts[i], max(1, left * loads[i] // mass), surplus)
            counts[i] = counts[i] + extra
            surplus = surplus - extra
    return np.array(counts)


def scatter_about(own_key, extent, deviation, most, shards=(), kind=jnp.bfloat16):
    array = deviation * jax.random.normal(own_key, extent, jnp.float32)
    if shards:
        array = array * steps_of(own_key, extent, shards, -0.22, 0.18)
    return jnp.clip(array, -most, most).astype(kind)


def setup_inputs(seed: int = 0) -> dict:
    splits = jax.random.split(jax.random.key(seed), 9)
    tokens = scatter_about(splits[0], (TOKENS, D), 1.0, 6.0, ((0, 16), (1, 2)))
    out_grad = scatter_about(splits[1], (TOKENS, D), 1.0, 6.0, ((0, 16), (1, 2)))
    route_probs = jnp.clip(0.099609375 + 0.9003906 * jax.random.uniform(splits[2], (TOKENS, TOP), jnp.float32) ** steps_of(splits[2], (TOKENS, TOP), ((0, 16),), -0.2, 0.2), 0.099609375, 1.0).astype(jnp.bfloat16)
    expert_ids_keys = jax.random.split(jax.random.fold_in(splits[3], 1), TOKENS // TOK_DEV)
    expert_ids_turns = jax.random.permutation(jax.random.fold_in(splits[3], 3), TOKENS // TOK_DEV)
    expert_ids = jax.vmap(lambda own, number: deal_out(jax.random.fold_in(splits[3], 2), own, number, TOK_DEV, EXPERTS, TOP, CAP, 2))(expert_ids_keys, expert_ids_turns).reshape((TOKENS, TOP))
    placement_map = jax.random.permutation(splits[4], EXPERTS).astype(jnp.int32)
    w_gate = scatter_about(splits[5], (N_DP, D, FF), D ** -0.5, 0.109375, ((0, 16), (2, 2)))
    w_up = scatter_about(splits[6], (N_DP, D, FF), D ** -0.5, 0.109375, ((0, 16), (2, 2)))
    w_down = scatter_about(splits[7], (N_DP, FF, D), FF ** -0.5, 0.109375, ((0, 16), (1, 2)))
    return {"tokens": tokens, "out_grad": out_grad, "route_probs": route_probs, "expert_ids": expert_ids, "placement_map": placement_map, "w_gate": w_gate, "w_up": w_up, "w_down": w_down}


SWISH_SLOPE = 1.702


def wave_layout(expert_ids, placement_map):
    code_value = placement_map[expert_ids].reshape(N_DP, TOK_DEV * TOP)
    in_wave = code_value % EXP_OWN == 0
    owner_of = code_value // EXP_OWN
    owner_range = jnp.arange(N_DP, dtype=jnp.int32)
    chosen = ((owner_of[:, :, None] == owner_range[None, None, :]) & in_wave[:, :, None]).astype(jnp.int32)
    before = jnp.cumsum(chosen, axis=1) - chosen
    slot_index = jnp.sum(before * chosen, axis=2).astype(jnp.int32)
    position = owner_range[:, None] * CAP + slot_index
    return in_wave, owner_of, position


def reference(tokens, out_grad, route_probs, expert_ids, placement_map, w_gate, w_up, w_down):
    in_wave, owner_of, position = wave_layout(expert_ids, placement_map)
    route_ids = jnp.arange(TOKENS * TOP, dtype=jnp.int32).reshape(N_DP, TOK_DEV * TOP)
    owner_row = jnp.where(in_wave, owner_of, N_DP).astype(jnp.int32)
    slot_route = jnp.full((N_DP, N_DP * CAP), -1, jnp.int32).at[owner_row, position].set(route_ids, mode="drop")
    flat_probs = route_probs.reshape(-1)
    zero_half = jnp.zeros((), jnp.bfloat16)
    block_width = FF // N_TENSOR

    def expert_backward(operands):
        gate_w, up_w, down_w, routes = operands
        row_valid = routes >= 0
        safe_route = jnp.where(row_valid, routes, 0).astype(jnp.int32)
        token_index = (safe_route // TOP).astype(jnp.int32)
        rows_x = jnp.where(row_valid[:, None], tokens[token_index], zero_half)
        rows_d = jnp.where(row_valid[:, None], out_grad[token_index], zero_half)
        prob_column = jnp.where(row_valid, flat_probs[safe_route], zero_half).astype(jnp.float32)[:, None]
        gate_pre = jnp.dot(rows_x, gate_w, preferred_element_type=jnp.float32)
        up_pre = jnp.dot(rows_x, up_w, preferred_element_type=jnp.float32)
        sig_gate = jax.nn.sigmoid(SWISH_SLOPE * gate_pre)
        active = (gate_pre * sig_gate * (up_pre + 1.0)).astype(jnp.bfloat16)
        down_back = jnp.dot(rows_d, down_w.T, preferred_element_type=jnp.float32)
        prob_sum = jnp.sum(active.astype(jnp.float32) * down_back, axis=1)
        delta_act = prob_column * down_back
        grad_gate_pre = (delta_act * (up_pre + 1.0) * (sig_gate + SWISH_SLOPE * gate_pre * sig_gate * (1.0 - sig_gate))).astype(jnp.bfloat16)
        grad_up_pre = (delta_act * gate_pre * sig_gate).astype(jnp.bfloat16)
        scaled_grad = (prob_column * rows_d.astype(jnp.float32)).astype(jnp.bfloat16)
        down_grad = jnp.dot(active.T, scaled_grad, preferred_element_type=jnp.float32).astype(jnp.bfloat16)
        gate_grad = jnp.dot(rows_x.T, grad_gate_pre, preferred_element_type=jnp.float32).astype(jnp.bfloat16)
        up_grad = jnp.dot(rows_x.T, grad_up_pre, preferred_element_type=jnp.float32).astype(jnp.bfloat16)
        input_total = jnp.zeros((routes.shape[0], D), jnp.float32)
        for block in range(N_TENSOR):
            lower = block * block_width
            upper = lower + block_width
            partial_rows = (jnp.dot(grad_gate_pre[:, lower:upper], gate_w[:, lower:upper].T, preferred_element_type=jnp.float32)
                            + jnp.dot(grad_up_pre[:, lower:upper], up_w[:, lower:upper].T, preferred_element_type=jnp.float32))
            input_total = input_total + partial_rows.astype(jnp.bfloat16).astype(jnp.float32)
        input_rows = input_total.astype(jnp.bfloat16)
        return gate_grad, up_grad, down_grad, input_rows, prob_sum.astype(jnp.bfloat16)

    gate_grad, up_grad, down_grad, back_rows, back_prob = lax.map(expert_backward, (w_gate, w_up, w_down, slot_route))
    flat_index = (jnp.where(in_wave, owner_of, 0) * (N_DP * CAP) + jnp.where(in_wave, position, 0)).reshape(-1).astype(jnp.int32)
    wave_flat = in_wave.reshape(-1)
    route_rows = jnp.where(wave_flat[:, None], back_rows.reshape(N_DP * N_DP * CAP, D)[flat_index], zero_half)
    input_grad = jnp.sum(route_rows.reshape(TOKENS, TOP, D).astype(jnp.float32), axis=1).astype(jnp.bfloat16)
    prob_grad = jnp.where(wave_flat, back_prob.reshape(-1)[flat_index], zero_half).reshape(TOKENS, TOP)
    return input_grad, gate_grad, up_grad, down_grad, prob_grad
```

```python
import jax
import jax.numpy as jnp
from jax import lax
from jax.sharding import PartitionSpec as P

EXP_OWN = 4


SWISH_SLOPE = 1.702


def swap(values):
    count = lax.axis_size("tensor")
    return lax.ppermute(values, "tensor", [(i, (i + 1) % count) for i in range(count)])


def join(mine, other, width):
    first = lax.axis_index("tensor") == 0
    low = jnp.where(first, mine, other)[:, :width]
    high = jnp.where(first, other, mine)[:, :width]
    return jnp.concatenate([low, high], axis=1)


def gather_columns(mine, width):
    if lax.axis_size("tensor") == 2:
        return join(mine, swap(mine), width)
    return lax.all_gather(mine[:, :width], "tensor", axis=1, tiled=True)


def scatter_columns(part, width):
    if lax.axis_size("tensor") != 2:
        return lax.psum_scatter(part, "tensor", scatter_dimension=1, tiled=True)
    first = lax.axis_index("tensor") == 0
    low, high = part[:, :width], part[:, width:]
    other = swap(jnp.where(first, high, low)).astype(jnp.float32)
    return (jnp.where(first, low, high).astype(jnp.float32) + other).astype(jnp.bfloat16)


def total(values):
    if lax.axis_size("tensor") == 2:
        return values + swap(values)
    return lax.psum(values, "tensor")


def shards(tokens, out_grad, route_probs, expert_ids, placement_map, w_gate, w_up, w_down):
    owners = lax.axis_size("dp")
    tok_rows, top_count = expert_ids.shape
    experts = placement_map.shape[0]
    per_owner = experts // owners
    capacity = 3 * tok_rows * top_count // (2 * EXP_OWN * owners)
    slots = capacity
    rows = owners * slots
    width = tokens.shape[1]
    half = jnp.bfloat16

    matches = expert_ids[:, :, None] == jnp.arange(experts, dtype=jnp.int32)[None, None, :]
    code_value = jnp.sum(jnp.where(matches, placement_map[None, None, :], 0), axis=-1)
    wave_codes = per_owner * jnp.arange(owners, dtype=jnp.int32)
    pick = code_value[:, :, None] == wave_codes[None, None, :]
    member = jnp.sum(pick.astype(jnp.float32), axis=1)
    probs_to = jnp.sum(
        jnp.where(pick, route_probs[:, :, None].astype(jnp.float32), 0.0), axis=1
    ).astype(half)
    earlier = (
        jnp.arange(tok_rows)[None, :] < jnp.arange(tok_rows)[:, None]
    ).astype(half)
    slot = lax.dot_general(
        member.astype(half), earlier, (((0,), (1,)), ((), ())), preferred_element_type=jnp.float32
    )
    key = jnp.where(member.T > 0, slot, -1.0).astype(jnp.int32)
    placed = key[:, None, :] == jnp.arange(slots, dtype=jnp.int32)[None, :, None]
    onehot = placed.astype(half).reshape(rows, tok_rows)

    def exchange(values):
        out = lax.all_to_all(
            values.reshape(owners, slots, values.shape[1]),
            "dp",
            split_axis=0,
            concat_axis=0,
            tiled=True,
        )
        return out.reshape(rows, values.shape[1])

    grad_and_prob = jnp.concatenate([out_grad, probs_to], axis=1)
    got_x = exchange(jnp.dot(onehot, tokens, preferred_element_type=jnp.float32).astype(half))
    send_d = jnp.dot(onehot, grad_and_prob, preferred_element_type=jnp.float32).astype(half)
    got_d = exchange(send_d)
    rows_x = gather_columns(got_x, width)
    rows_d = gather_columns(got_d, width)
    mine = jnp.arange(owners) == lax.axis_index("dp")
    prob_column = jnp.sum(
        jnp.where(mine[None, :], got_d[:, width:].astype(jnp.float32), 0.0), axis=1, keepdims=True
    )

    gate_w = w_gate[0]
    up_w = w_up[0]
    down_w = w_down[0]
    contract_cols = (((1,), (1,)), ((), ()))
    contract_rows = (((0,), (0,)), ((), ()))
    gate_pre = jnp.dot(rows_x, gate_w, preferred_element_type=jnp.float32)
    up_pre = jnp.dot(rows_x, up_w, preferred_element_type=jnp.float32)
    sig_gate = jax.nn.sigmoid(SWISH_SLOPE * gate_pre)
    active = (gate_pre * sig_gate * (up_pre + 1.0)).astype(half)
    down_back = lax.dot_general(rows_d, down_w, contract_cols, preferred_element_type=jnp.float32)
    slice_sum = jnp.sum(active.astype(jnp.float32) * down_back, axis=1)
    prob_sum = total(slice_sum)
    delta_act = prob_column * down_back
    grad_gate_pre = (
        delta_act
        * (up_pre + 1.0)
        * (sig_gate + SWISH_SLOPE * gate_pre * sig_gate * (1.0 - sig_gate))
    ).astype(half)
    grad_up_pre = (delta_act * gate_pre * sig_gate).astype(half)
    scaled_grad = (prob_column * rows_d.astype(jnp.float32)).astype(half)
    input_part = lax.dot_general(
        grad_gate_pre, gate_w, contract_cols, preferred_element_type=jnp.float32
    ) + lax.dot_general(grad_up_pre, up_w, contract_cols, preferred_element_type=jnp.float32)
    rounded_part = lax.optimization_barrier(input_part.astype(half))
    input_rows = scatter_columns(rounded_part, width)
    back = exchange(jnp.concatenate([input_rows, prob_sum.astype(half)[:, None]], axis=1))

    down_grad = lax.dot_general(
        active, scaled_grad, contract_rows, preferred_element_type=jnp.float32
    ).astype(half)
    gate_grad = lax.dot_general(
        rows_x, grad_gate_pre, contract_rows, preferred_element_type=jnp.float32
    ).astype(half)
    up_grad = lax.dot_general(
        rows_x, grad_up_pre, contract_rows, preferred_element_type=jnp.float32
    ).astype(half)

    combined = lax.dot_general(onehot, back, contract_rows, preferred_element_type=jnp.float32)
    input_grad = combined[:, :width].astype(half)
    back_prob = back[:, width].astype(jnp.float32).reshape(owners, slots)
    prob_to = jnp.sum(jnp.where(placed, back_prob[:, :, None], 0.0), axis=1).T
    prob_grad = jnp.sum(jnp.where(pick, prob_to[:, None, :], 0.0), axis=2).astype(half)
    return (input_grad, gate_grad[None], up_grad[None], down_grad[None], prob_grad)


def solution(mesh):
    in_specs = (
        P("dp", "tensor"),
        P("dp", "tensor"),
        P("dp", None),
        P("dp", None),
        P(),
        P("dp", None, "tensor"),
        P("dp", None, "tensor"),
        P("dp", "tensor", None),
    )
    out_specs = (
        P("dp", "tensor"),
        P("dp", None, "tensor"),
        P("dp", None, "tensor"),
        P("dp", "tensor", None),
        P("dp", None),
    )
    return jax.shard_map(shards, mesh=mesh, in_specs=in_specs, out_specs=out_specs, check_vma=False)
```
